512 devices in a mesh: grp: 16 (over x, z_lo), blk: 32 (over y, z_hi, core).
Axes of the slice: x: 4, y: 8, z: 8 (z_hi: 2, z_lo: 4; z = z_hi * 4 + z_lo), core: 2. Of those that a mesh axis runs over, the one named last changes fastest.
Arguments:
- users: float32 [131072, 256], P(('grp', 'blk')), may hold values from -0.125 to 0.125
- user_momentum: float32 [131072, 256], P(('grp', 'blk')), may hold values from -6 to 6
- items: float32 [8192, 256], P('blk'), may hold values from -0.125 to 0.125
- item_momentum: float32 [8192, 256], P('blk'), may hold values from -6 to 6
- ratings: float32 [131072, 6, 256], P(('grp', 'blk')), may hold values from -6 to 6
- rating_mask: int32 [131072, 6, 256], P(('grp', 'blk')), may hold values 0 or 1
- tile_occupied: int32 [1024, 6, 2], P(('grp', 'blk')), may hold values 0 or 1
- stagger: int32 [16], replicated, may hold values from 0 to 31
Outputs:
- new_users: float32 [131072, 256], P(('grp', 'blk'))
- new_user_momentum: float32 [131072, 256], P(('grp', 'blk'))
- new_items: float32 [8192, 256], P(('blk', 'grp'))
The draws below stay inside these ranges and needn't reach their ends.
All inputs are finite; a program needn't handle non-finite values. No bound on the sum of `rating_mask` or of `tile_occupied` on one device may be relied on, other than what follows from the above.
Results may differ from the reference program's by a relative error of at most 0.0003.
Values sent between devices are 32-bit elements; how exact they have to be, the bound alone decides.
A program may use at most 64 MiB of HBM per device.

```python
import jax
import jax.numpy as jnp
from jax import lax

R = 256
TILE = 128
USR_DEV = 256
IT_DEV = 256
STEPS = 6
PASSES = 2
USERS = 131072
ITEMS = 8192
N_GRP = 16
N_BLK = 32


def touch_ends(array, key, smallest, high):
    place = [jax.random.randint(jax.random.fold_in(key, axis), (), 0, length) for axis, length in enumerate(array.shape)]
    longest = array.shape.index(max(array.shape))
    next_to = place[:longest] + [(place[longest] + 1) % array.shape[longest]] + place[longest + 1:]
    return array.at[tuple(place)].set(smallest).at[tuple(next_to)].set(high)


def level_of(own_key, extent, cuts, smallest, largest):
    gain, own = 1.0, jax.random.fold_in(own_key, 6)
    for position, parts in cuts:
        steps = jnp.exp(jax.random.uniform(jax.random.fold_in(own, position), (parts,), jnp.float32, smallest / len(cuts), largest / len(cuts)))
        gain = gain * jnp.repeat(steps, extent[position] // parts).reshape([-1 if axis == position else 1 for axis in range(len(extent))])
    return gain


def normal_values(rng, dims, deviation, reach, pieces=(), held_as=jnp.bfloat16):
    factor_of = level_of(rng, dims, pieces, -0.22, 0.18) if pieces else 1.0
    array = jax.random.normal(rng, dims, jnp.float32) * deviation * factor_of
    return jnp.minimum(jnp.maximum(array, -reach), reach).astype(held_as)


def setup_inputs(seed: int = 0) -> dict:
    seeds = jax.random.split(jax.random.key(seed), 9)
    users = normal_values(seeds[0], (USERS, R), 0.05, 0.125, ((0, 512),), jnp.float32)
    user_momentum = normal_values(seeds[1], (USERS, R), 1.0, 6.0, ((0, 512),), jnp.float32)
    items = normal_values(seeds[2], (ITEMS, R), 0.05, 0.125, ((0, 32),), jnp.float32)
    item_momentum = normal_values(seeds[3], (ITEMS, R), 1.0, 6.0, ((0, 32),), jnp.float32)
    ratings = normal_values(seeds[4], (USERS, STEPS, IT_DEV), 1.0, 6.0, ((0, 512),), jnp.float32)
    rating_mask = touch_ends((jax.random.randint(seeds[5], (USERS, STEPS, IT_DEV), 0, 2) < 1).astype(jnp.int32), jax.random.fold_in(seeds[5], 1), 0, 1)
    tile_occupied = touch_ends((jax.random.randint(seeds[6], (USERS // TILE, STEPS, IT_DEV // TILE), 0, 4) < 3).astype(jnp.int32), jax.random.fold_in(seeds[6], 1), 0, 1)
    stagger = touch_ends(jax.random.randint(seeds[7], (N_GRP,), 0, N_BLK), jax.random.fold_in(seeds[7], 1), 0, N_BLK - 1).astype(jnp.int32)
    return {"users": users, "user_momentum": user_momentum, "items": items, "item_momentum": item_momentum, "ratings": ratings, "rating_mask": rating_mask, "tile_occupied": tile_occupied, "stagger": stagger}


momentum_decay = 0.9
shrinkage = 0.05
rate_scale = 0.8


def reference(users, user_momentum, items, item_momentum, ratings, rating_mask, tile_occupied, stagger):
    rows = N_BLK * USR_DEV
    user_tiles = USR_DEV // TILE
    item_tiles = IT_DEV // TILE
    user_rate = rate_scale / IT_DEV
    item_rate = rate_scale / USR_DEV
    base_rows = items.reshape(N_BLK, IT_DEV, R)
    base_mom = item_momentum.reshape(N_BLK, IT_DEV, R)
    highest = lax.Precision.HIGHEST

    def group(total, index):
        offset = stagger[index]
        start = (index * rows).astype(jnp.int32)
        user_rows = lax.dynamic_slice_in_dim(users, start, rows, 0).reshape(N_BLK, USR_DEV, R)
        user_mom = lax.dynamic_slice_in_dim(user_momentum, start, rows, 0).reshape(N_BLK, USR_DEV, R)
        target = lax.dynamic_slice_in_dim(ratings, start, rows, 0).reshape(N_BLK, USR_DEV, STEPS, IT_DEV)
        marks = lax.dynamic_slice_in_dim(rating_mask, start, rows, 0).reshape(N_BLK, user_tiles, TILE, STEPS, item_tiles, TILE)
        tile_start = (index * (rows // TILE)).astype(jnp.int32)
        tiles = lax.dynamic_slice_in_dim(tile_occupied, tile_start, rows // TILE, 0).reshape(N_BLK, user_tiles, 1, STEPS, item_tiles, 1)
        weight = (marks * tiles).reshape(N_BLK, USR_DEV, STEPS, IT_DEV).astype(jnp.float32)
        item_rows = jnp.roll(base_rows, -offset, axis=0)
        item_mom = jnp.roll(base_mom, -offset, axis=0)
        for step in range(STEPS):
            for repeat in range(PASSES):
                predicted = jnp.einsum('bur,bir->bui', user_rows, item_rows, precision=highest)
                residue = weight[:, :, step, :] * (predicted - target[:, :, step, :])
                user_grad = jnp.einsum('bui,bir->bur', residue, item_rows, precision=highest) + shrinkage * user_rows
                item_grad = jnp.einsum('bui,bur->bir', residue, user_rows, precision=highest) + shrinkage * item_rows
                user_mom = momentum_decay * user_mom + user_grad
                item_mom = momentum_decay * item_mom + item_grad
                user_rows = user_rows - user_rate * user_mom
                item_rows = item_rows - item_rate * item_mom
            if step + 1 < STEPS:
                item_rows = jnp.roll(item_rows, 1, axis=0)
                item_mom = jnp.roll(item_mom, 1, axis=0)
        returned = jnp.roll(item_rows, offset - (STEPS - 1), axis=0)
        return total + (returned - base_rows), (user_rows.reshape(rows, R), user_mom.reshape(rows, R))

    start_total = jnp.zeros((N_BLK, IT_DEV, R), jnp.float32)
    total, outs = lax.scan(group, start_total, jnp.arange(N_GRP, dtype=jnp.int32))
    new_users = outs[0].reshape(USERS, R)
    new_mom = outs[1].reshape(USERS, R)
    new_items = items + (total / N_GRP).reshape(ITEMS, R)
    return new_users, new_mom, new_items
```

```python
import functools

import jax
import jax.numpy as jnp
from jax import lax
from jax.experimental import pallas as pl
from jax.experimental.pallas import tpu as pltpu
from jax.sharding import PartitionSpec as P

TILE = 128
STEPS = 6
PASSES = 2
GEOM = (4, 4, 8)
YC = 2
LANES = 128

momentum_decay = 0.9
shrinkage = 0.05
rate_scale = 0.8

MESH = pl.DeviceIdType.MESH
f32 = jnp.float32
bf16 = jnp.bfloat16


def split2(a):
    hi = a.astype(bf16)
    return hi, (a - hi.astype(f32)).astype(bf16)


def dot3(a, b, dims):
    def one(p, q):
        return lax.dot_general(p, q, (dims, ((), ())), preferred_element_type=f32)

    return one(a[0], b[0]) + (one(a[0], b[1]) + one(a[1], b[0]))


def kernel(
    stag, tiles, users, umom, items, imom, ratings, mask,
    out_u, out_p, out_i,
    own, got, outbox, hold, raw_m, rat, wgt,
    fin, c1_out, c1_in, c2_out, c2_in, c3_out, c3_in,
    load_sem, s1, r1, s2, r2, ring_s, ring_r, sc, rc,
):
    nx, nl, ny = GEOM
    nz = 2 * nl
    ng, nb = nx * nl, ny * 4
    rank = out_u.shape[1]
    halves = rank // LANES
    n_items = own.shape[1]
    n_users = out_u.shape[0]
    prow = got.shape[2]
    g = lax.axis_index("grp")
    b = lax.axis_index("blk")
    x, y, z, c = g // nl, b // 4, (b // 2) % 2 * nl + g % nl, b % 2

    def dev(xx, yy, zz, cc):
        return (xx * nl + zz % nl, (yy * 2 + zz // nl) * 2 + cc)

    def piece_of(xx, yy, zz, cc):
        return ((xx * nl + zz % nl) * 2 + cc) * YC + yy % YC

    def part(ref, p):
        row = pl.multiple_of(p // halves * prow, prow)
        col = pl.multiple_of(p % halves * LANES, LANES)
        return ref.at[:, pl.ds(row, prow), pl.ds(col, LANES)]

    loads = []
    for i, (src, dst) in enumerate(
        (
            (items, own.at[0]),
            (imom, own.at[1]),
            (ratings, rat),
            (mask, raw_m),
            (users, out_u),
            (umom, out_p),
        )
    ):
        copy = pltpu.make_async_copy(src, dst, load_sem.at[i])
        copy.start()
        loads.append(copy)

    def offsets(xs, cs):
        for dz in range(nl):
            zoff = dz if 2 * dz < nl else dz - nl
            if 2 * dz == nl:
                zoff = dz * (1 - 2 * (xs % 2))
            for dy in range(YC):
                yoff = dy
                if 2 * dy == YC:
                    yoff = dy * (1 - 2 * cs)
                yield dz, dy, zoff, yoff

    def second(sign):
        for dx in range(nx):
            for dc in range(2):
                other = ((x + dx) % nx, (c + dc) % 2)
                sx, sc_ = other if sign > 0 else (x, c)
                for dz, dy, zoff, yoff in offsets(sx, sc_):
                    at = (
                        other[0],
                        (y + sign * yoff + ny) % ny,
                        (z + sign * zoff + nz) % nz,
                        other[1],
                    )
                    yield (dx == 0 and dz == 0), (dx + dc + dz + dy == 0), at

    barrier = pltpu.get_barrier_semaphore()
    count = 0
    greet = [(g, (b + d) % nb) for d in range(1, nb)]
    greet += [dev(x, yy, nz - 1 - z, cc) for yy in range(ny) for cc in range(2)]
    greet += [dev(*at) for near, _, at in second(1) if not near]
    greet += [((g + d) % ng, b) for d in range(1, ng)]
    for who in greet:
        pl.semaphore_signal(barrier, inc=1, device_id=who, device_id_type=MESH)
        count += 1
    loads[0].wait()
    loads[1].wait()
    pl.semaphore_wait(barrier, count)

    mine = piece_of(x, y, z, c)
    for dy in range(ny):
        for flip in range(2):
            for dc in range(2):
                if dy + flip + dc == 0:
                    continue
                yy, zz, cc = (y + dy) % ny, (nz - 1 - z if flip else z), (c + dc) % 2
                pltpu.make_async_remote_copy(
                    src_ref=part(own, piece_of(x, yy, zz, cc)),
                    dst_ref=got.at[b],
                    send_sem=s1,
                    recv_sem=r1,
                    device_id=dev(x, yy, zz, cc),
                    device_id_type=MESH,
                ).start()
    got[b] = part(own, mine)[...]

    loads[2].wait()
    loads[3].wait()
    for s in range(STEPS):
        for ut in range(n_users // TILE):
            for it in range(n_items // TILE):
                ur, ir = pl.ds(ut * TILE, TILE), pl.ds(it * TILE, TILE)
                wgt[s, ur, ir] = (raw_m[s, ur, ir] * tiles[s, ut, it]).astype(f32)
    loads[4].wait()
    loads[5].wait()

    several = got.at[pl.ds(0, nb - 1)]
    pltpu.make_async_copy(several, several, r1).wait()

    outs = list(second(-1))
    k = 0
    sends = []
    for _, self_, at in outs:
        gd, bd = dev(*at)
        at_block = (bd + stag[gd]) % nb
        if self_:
            part(hold.at[0], mine)[...] = got[at_block]
        else:
            outbox[k] = got[at_block]
            sends.append((k, (gd, bd)))
            k += 1
    for k, who in sends:
        pltpu.make_async_remote_copy(
            src_ref=outbox.at[k],
            dst_ref=part(hold.at[0], mine),
            send_sem=s2,
            recv_sem=r2,
            device_id=who,
            device_id_type=MESH,
        ).start()
    sent = outbox.at[pl.ds(0, len(sends))]
    pltpu.make_async_copy(sent, sent, r2).wait()

    def onward(s):
        return pltpu.make_async_remote_copy(
            src_ref=hold.at[s],
            dst_ref=hold.at[s + 1],
            send_sem=ring_s.at[s],
            recv_sem=ring_r.at[s],
            device_id=(g, (b + 1) % nb),
            device_id_type=MESH,
        )

    user_rate = rate_scale / n_items
    item_rate = rate_scale / n_users

    def step(s, carry):
        @pl.when(s > 0)
        def _():
            onward(s - 1).wait_recv()

        for _ in range(PASSES):
            u, v = out_u[...], hold[s, 0]
            us, vs = split2(u), split2(v)
            pred = dot3(us, vs, ((1,), (1,)))
            res = split2(wgt[s] * (pred - rat[s]))
            ugrad = dot3(res, vs, ((1,), (0,))) + shrinkage * u
            igrad = dot3(res, us, ((0,), (0,))) + shrinkage * v
            p = momentum_decay * out_p[...] + ugrad
            m = momentum_decay * hold[s, 1] + igrad
            out_p[...] = p
            out_u[...] = u - user_rate * p
            hold[s, 1] = m
            hold[s, 0] = v - item_rate * m

        @pl.when(s < STEPS - 1)
        def _():
            onward(s).start()

        return carry

    lax.fori_loop(0, STEPS, step, 0)

    per = n_items // ng
    for h in range(halves):
        fin[pl.ds(h * n_items, n_items), :] = hold[STEPS - 1, 0, :, pl.ds(h * LANES, LANES)]
    for t in range(nb):
        r, h = t % per, t // per
        c1_out[t] = fin[pl.ds(h * n_items + r, ng, stride=per), :]
    for d in range(1, nb):
        t = (b + d) % nb
        pltpu.make_async_remote_copy(
            src_ref=c1_out.at[t],
            dst_ref=c1_in.at[b],
            send_sem=sc.at[0],
            recv_sem=rc.at[0],
            device_id=(g, t),
            device_id_type=MESH,
        ).start()
    c1_in[b] = c1_out[b]
    some = c1_in.at[pl.ds(0, nb - 1)]
    pltpu.make_async_copy(some, some, rc.at[0]).wait()
    shift = nb - stag[g] + STEPS - 1
    for j in range(nb):
        c2_out[pl.ds(j, ng, stride=nb), :] = c1_in[(j + shift) % nb]
    for d in range(1, ng):
        t = (g + d) % ng
        pltpu.make_async_remote_copy(
            src_ref=c2_out.at[pl.ds(pl.multiple_of(t * nb, nb), nb)],
            dst_ref=c2_in.at[g],
            send_sem=sc.at[1],
            recv_sem=rc.at[1],
            device_id=(t, b),
            device_id_type=MESH,
        ).start()
    c2_in[g] = c2_out[pl.ds(pl.multiple_of(g * nb, nb), nb), :]
    some2 = c2_in.at[pl.ds(0, ng - 1)]
    pltpu.make_async_copy(some2, some2, rc.at[1]).wait()
    total = c2_in[0]
    for i in range(1, ng):
        total = total + c2_in[i]
    total = total / ng
    for j in range(nb):
        c3_out[j] = total[j : j + 1]
    for d in range(1, nb):
        t = (b + d) % nb
        pltpu.make_async_remote_copy(
            src_ref=c3_out.at[t],
            dst_ref=c3_in.at[b],
            send_sem=sc.at[2],
            recv_sem=rc.at[2],
            device_id=(g, t),
            device_id_type=MESH,
        ).start()
    c3_in[b] = c3_out[b]

    pltpu.make_async_copy(several, several, s1).wait()
    pltpu.make_async_copy(sent, sent, s2).wait()
    for s in range(STEPS - 1):
        onward(s).wait_send()
    pltpu.make_async_copy(some, some, sc.at[0]).wait()
    pltpu.make_async_copy(some2, some2, sc.at[1]).wait()
    some3 = c3_in.at[pl.ds(0, nb - 1)]
    pltpu.make_async_copy(some3, some3, sc.at[2]).wait()
    pltpu.make_async_copy(some3, some3, rc.at[2]).wait()
    for t in range(nb):
        r, h = t % per, t // per
        out_i[pl.ds(r, 1), pl.ds(h * LANES, LANES)] = c3_in[t]


def on_device(
    users, user_momentum, items, item_momentum, ratings, rating_mask, tile_occupied, stagger
):
    nx, nl, ny = GEOM
    ng, nb = nx * nl, ny * 4
    n_users, rank = users.shape
    n_items = items.shape[0]
    pieces = ng * 2 * YC
    prow = n_items * (rank // LANES) // pieces
    vm = pl.BlockSpec(memory_space=pltpu.VMEM)
    sm = pl.BlockSpec(memory_space=pltpu.SMEM)
    hbm = pl.BlockSpec(memory_space=pl.ANY)
    dma = pltpu.SemaphoreType.DMA
    return pl.pallas_call(
        kernel,
        out_shape=(
            jax.ShapeDtypeStruct(users.shape, f32),
            jax.ShapeDtypeStruct(users.shape, f32),
            jax.ShapeDtypeStruct((n_items // ng, rank), f32),
        ),
        in_specs=[sm, sm] + [hbm] * 6,
        out_specs=(vm, vm, vm),
        scratch_shapes=[
            pltpu.VMEM((2, n_items, rank), f32),
            pltpu.VMEM((nb, 2, prow, LANES), f32),
            pltpu.VMEM((pieces, 2, prow, LANES), f32),
            pltpu.VMEM((STEPS, 2, n_items, rank), f32),
            pltpu.VMEM((STEPS, n_users, n_items), jnp.int32),
            pltpu.VMEM((STEPS, n_users, n_items), f32),
            pltpu.VMEM((STEPS, n_users, n_items), f32),
            pltpu.VMEM((n_items * (rank // LANES), LANES), f32),
            pltpu.VMEM((nb, ng, LANES), f32),
            pltpu.VMEM((nb, ng, LANES), f32),
            pltpu.VMEM((ng * nb, LANES), f32),
            pltpu.VMEM((ng, nb, LANES), f32),
            pltpu.VMEM((nb, 1, LANES), f32),
            pltpu.VMEM((nb, 1, LANES), f32),
            dma((6,)),
            dma,
            dma,
            dma,
            dma,
            dma((STEPS - 1,)),
            dma((STEPS - 1,)),
            dma((3,)),
            dma((3,)),
        ],
        compiler_params=pltpu.CompilerParams(
            collective_id=0, has_side_effects=True, vmem_limit_bytes=60 * 2**20
        ),
        name="window",
    )(
        stagger,
        jnp.transpose(tile_occupied, (1, 0, 2)),
        users,
        user_momentum,
        items,
        item_momentum,
        jnp.transpose(ratings, (1, 0, 2)),
        jnp.transpose(rating_mask, (1, 0, 2)),
    )


def solution(mesh):
    in_specs = (
        P(("grp", "blk"), None),
        P(("grp", "blk"), None),
        P("blk", None),
        P("blk", None),
        P(("grp", "blk"), None, None),
        P(("grp", "blk"), None, None),
        P(("grp", "blk"), None, None),
        P(),
    )
    out_specs = (P(("grp", "blk"), None), P(("grp", "blk"), None), P(("blk", "grp"), None))
    return jax.shard_map(
        on_device, mesh=mesh, in_specs=in_specs, out_specs=out_specs, check_vma=False
    )
```

```python
import functools

import jax
import jax.numpy as jnp
from jax import lax
from jax.experimental import pallas as pl
from jax.experimental.pallas import tpu as pltpu
from jax.sharding import PartitionSpec as P

TILE = 128
STEPS = 6
PASSES = 2
GEOM = (4, 4, 8)
YC_OPEN = 4
YC_CLOSE = 2
LANES = 128

momentum_decay = 0.9
shrinkage = 0.05
rate_scale = 0.8

MESH = pl.DeviceIdType.MESH
f32 = jnp.float32
bf16 = jnp.bfloat16


def split2(a):
    hi = a.astype(bf16)
    return hi, (a - hi.astype(f32)).astype(bf16)


def dot3(a, b, dims):
    def one(p, q):
        return lax.dot_general(p, q, (dims, ((), ())), preferred_element_type=f32)

    return one(a[0], b[0]) + (one(a[0], b[1]) + one(a[1], b[0]))


def kernel(
    stag, tiles, users, umom, items, imom, ratings, mask,
    out_u, out_p, out_i,
    own, got, outbox, hold, raw_m, rat, wgt,
    c1_in, c2_out, c2_in,
    load_sem, s1, r1, s2, r2, ring_s, ring_r, sc, rc,
):
    nx, nl, ny = GEOM
    nz = 2 * nl
    ng, nb = nx * nl, ny * 4
    rank = out_u.shape[1]
    halves = rank // LANES
    n_items = own.shape[1]
    n_users = out_u.shape[0]
    planes, prow = got.shape[1], got.shape[2]
    g = lax.axis_index("grp")
    b = lax.axis_index("blk")
    x, y, z, c = g // nl, b // 4, (b // 2) % 2 * nl + g % nl, b % 2

    def dev(xx, yy, zz, cc):
        return (xx * nl + zz % nl, (yy * 2 + zz // nl) * 2 + cc)

    def rows_cols(xx, yy, zz, cc):
        row = ((xx * nl + zz % nl) * 2 + cc) * prow
        col = yy % halves * LANES
        return pl.ds(pl.multiple_of(row, prow), prow), pl.ds(pl.multiple_of(col, LANES), LANES)

    def part(ref, at):
        plane = at[1] % YC_OPEN // halves * planes
        return ref.at[(pl.ds(plane, planes), *rows_cols(*at))]

    loads = []
    for i, (src, dst) in enumerate(
        (
            (items, own.at[0]),
            (imom, own.at[1]),
            (ratings, rat),
            (mask, raw_m),
            (users, out_u),
            (umom, out_p),
        )
    ):
        copy = pltpu.make_async_copy(src, dst, load_sem.at[i])
        copy.start()
        loads.append(copy)

    def pairs(classes, sign):
        found = [((x, y, z, 1 - c), True)]
        for cc in (1, 0):
            for dx in range(nx):
                xx = (x + dx) % nx
                hx, hc = (xx, cc) if sign > 0 else (x, c)
                for dz in range(nl):
                    zoff = dz if 2 * dz < nl else dz - nl
                    if 2 * dz == nl:
                        zoff = dz * (1 - 2 * (hx % 2))
                    for dy in range(classes):
                        yoff = dy if 2 * dy < classes else dy - classes
                        if 2 * dy == classes:
                            yoff = dy * (1 - 2 * hc)
                        if dx + dz + dy:
                            yy = (y + sign * yoff + ny) % ny
                            zz = (z + sign * zoff + nz) % nz
                            found.append(((xx, yy, zz, cc), dx + dz == 0))
        return found

    for gg in range(ng):
        c1_in[gg] = jnp.zeros(c1_in.shape[1:], f32)

    barrier = pltpu.get_barrier_semaphore()
    greet = [(g, (b + d) % nb) for d in range(1, nb)]
    greet += [dev(x, yy, nz - 1 - z, cc) for yy in range(ny) for cc in range(2)]
    greet += [dev(*at) for at, near in pairs(YC_OPEN, 1) if not near]
    greet += [dev(*at) for at, near in pairs(YC_CLOSE, -1) if not near]
    for who in greet:
        pl.semaphore_signal(barrier, inc=1, device_id=who, device_id_type=MESH)
    loads[0].wait()
    loads[1].wait()
    pl.semaphore_wait(barrier, len(greet))

    me = (x, y, z, c)
    for dy in sorted(range(ny), key=lambda d: -min(d, ny - d)):
        for flip in range(2):
            for dc in range(2):
                if dy + flip + dc == 0:
                    continue
                at = (x, (y + dy) % ny, (nz - 1 - z if flip else z), (c + dc) % 2)
                pltpu.make_async_remote_copy(
                    src_ref=part(own, at),
                    dst_ref=got.at[b],
                    send_sem=s1,
                    recv_sem=r1,
                    device_id=dev(*at),
                    device_id_type=MESH,
                ).start()
    got[b] = part(own, me)[...]

    for copy in loads[2:]:
        copy.wait()
    for s in range(STEPS):
        for ut in range(n_users // TILE):
            for it in range(n_items // TILE):
                ur, ir = pl.ds(ut * TILE, TILE), pl.ds(it * TILE, TILE)
                wgt[s, ur, ir] = (raw_m[s, ur, ir] * tiles[ut, it, s]).astype(f32)

    several = got.at[pl.ds(0, nb - 1)]
    pltpu.make_async_copy(several, several, r1).wait()

    part(hold.at[0], me)[...] = got[(b + stag[g]) % nb]
    outs = [dev(*at) for at, _ in pairs(YC_OPEN, -1)]
    for k, (gd, bd) in enumerate(outs):
        outbox[k] = got[(bd + stag[gd]) % nb]
    for k, who in enumerate(outs):
        pltpu.make_async_remote_copy(
            src_ref=outbox.at[k],
            dst_ref=part(hold.at[0], me),
            send_sem=s2,
            recv_sem=r2,
            device_id=who,
            device_id_type=MESH,
        ).start()
    sent = outbox.at[pl.ds(0, len(outs))]
    pltpu.make_async_copy(sent, sent, r2).wait()

    def onward(s):
        return pltpu.make_async_remote_copy(
            src_ref=hold.at[s],
            dst_ref=hold.at[s + 1],
            send_sem=ring_s.at[s],
            recv_sem=ring_r.at[s],
            device_id=(g, (b + 1) % nb),
            device_id_type=MESH,
        )

    user_rate = rate_scale / n_items
    item_rate = rate_scale / n_users

    def step(s, carry):
        @pl.when(s > 0)
        def _():
            onward(s - 1).wait_recv()

        for _ in range(PASSES):
            u, v = out_u[...], hold[s, 0]
            us, vs = split2(u), split2(v)
            pred = dot3(us, vs, ((1,), (1,)))
            res = split2(wgt[s] * (pred - rat[s]))
            ugrad = dot3(res, vs, ((1,), (0,))) + shrinkage * u
            igrad = dot3(res, us, ((0,), (0,))) + shrinkage * v
            p = momentum_decay * out_p[...] + ugrad
            m = momentum_decay * hold[s, 1] + igrad
            out_p[...] = p
            out_u[...] = u - user_rate * p
            hold[s, 1] = m
            hold[s, 0] = v - item_rate * m

        @pl.when(s < STEPS - 1)
        def _():
            onward(s).start()

        return carry

    lax.fori_loop(0, STEPS, step, 0)

    last = hold.at[STEPS - 1, 0]
    for at, _ in pairs(YC_CLOSE, 1):
        pltpu.make_async_remote_copy(
            src_ref=last.at[rows_cols(*at)],
            dst_ref=c1_in.at[g, b],
            send_sem=sc.at[0],
            recv_sem=rc.at[0],
            device_id=dev(*at),
            device_id_type=MESH,
        ).start()
    c1_in[g, b] = last[rows_cols(*me)]
    pieces = ng * 2 * YC_CLOSE
    some = outbox.at[pl.ds(0, (pieces - 1) // planes)] if planes == 1 else None
    pltpu.make_async_copy(some, some, rc.at[0]).wait()
    shifts = [nb - stag[gg] + STEPS - 1 for gg in range(ng)]
    for j in range(nb):
        total = c1_in[0, (j + shifts[0]) % nb]
        for gg in range(1, ng):
            total = total + c1_in[gg, (j + shifts[gg]) % nb]
        c2_out[j] = total * (1 / ng)
    for d in sorted(range(1, nb), key=lambda d: -min(d, nb - d)):
        t = (b + d) % nb
        pltpu.make_async_remote_copy(
            src_ref=c2_out.at[t],
            dst_ref=c2_in.at[b],
            send_sem=sc.at[1],
            recv_sem=rc.at[1],
            device_id=(g, t),
            device_id_type=MESH,
        ).start()
    c2_in[b] = c2_out[b]

    pltpu.make_async_copy(several, several, s1).wait()
    pltpu.make_async_copy(sent, sent, s2).wait()
    for s in range(STEPS - 1):
        onward(s).wait_send()
    pltpu.make_async_copy(some, some, sc.at[0]).wait()
    some2 = c2_in.at[pl.ds(0, nb - 1)]
    pltpu.make_async_copy(some2, some2, sc.at[1]).wait()
    pltpu.make_async_copy(some2, some2, rc.at[1]).wait()
    for cc in range(2):
        for h in range(halves):
            held = [c2_in[(yy * 2 + zh) * 2 + cc] for yy in range(h, ny, halves) for zh in range(2)]
            out_i[pl.ds(cc * prow, prow), pl.ds(h * LANES, LANES)] = sum(held[1:], held[0])


def copy_out(*refs):
    n = len(refs) // 2
    for src, dst in zip(refs[:n], refs[n:]):
        dst[...] = src[...]


def on_device(
    users, user_momentum, items, item_momentum, ratings, rating_mask, tile_occupied, stagger
):
    nx, nl, ny = GEOM
    ng, nb = nx * nl, ny * 4
    n_users, rank = users.shape
    n_items = items.shape[0]
    pieces = ng * 2 * YC_OPEN
    planes = 4 // YC_OPEN
    prow = n_items // (ng * 2)
    vm = pl.BlockSpec(memory_space=pltpu.VMEM)
    sm = pl.BlockSpec(memory_space=pltpu.SMEM)
    hbm = pl.BlockSpec(memory_space=pl.ANY)
    dma = pltpu.SemaphoreType.DMA
    results = pl.pallas_call(
        kernel,
        out_shape=(
            jax.ShapeDtypeStruct(users.shape, f32),
            jax.ShapeDtypeStruct(users.shape, f32),
            jax.ShapeDtypeStruct((n_items // ng, rank), f32),
        ),
        in_specs=[sm, sm] + [hbm] * 6,
        out_specs=(vm, vm, vm),
        scratch_shapes=[
            pltpu.VMEM((2, n_items, rank), f32),
            pltpu.VMEM((nb, planes, prow, LANES), f32),
            pltpu.VMEM((pieces, planes, prow, LANES), f32),
            pltpu.VMEM((STEPS, 2, n_items, rank), f32),
            pltpu.VMEM((STEPS, n_users, n_items), jnp.int32),
            pltpu.VMEM((STEPS, n_users, n_items), f32),
            pltpu.VMEM((STEPS, n_users, n_items), f32),
            pltpu.VMEM((ng, nb, prow, LANES), f32),
            pltpu.VMEM((nb, prow, LANES), f32),
            pltpu.VMEM((nb, prow, LANES), f32),
            dma((6,)),
            dma,
            dma,
            dma,
            dma,
            dma((STEPS - 1,)),
            dma((STEPS - 1,)),
            dma((2,)),
            dma((2,)),
        ],
        compiler_params=pltpu.CompilerParams(
            collective_id=0, has_side_effects=True, vmem_limit_bytes=60 * 2**20
        ),
        name="window",
    )(
        stagger,
        jnp.transpose(tile_occupied, (0, 2, 1)),
        users,
        user_momentum,
        items,
        item_momentum,
        jnp.transpose(ratings, (1, 0, 2)),
        jnp.transpose(rating_mask, (1, 0, 2)),
    )
    return pl.pallas_call(
        copy_out,
        out_shape=tuple(jax.ShapeDtypeStruct(r.shape, r.dtype) for r in results),
        in_specs=[vm] * 3,
        out_specs=(vm,) * 3,
        name="results",
    )(*results)


def solution(mesh):
    in_specs = (
        P(("grp", "blk"), None),
        P(("grp", "blk"), None),
        P("blk", None),
        P("blk", None),
        P(("grp", "blk"), None, None),
        P(("grp", "blk"), None, None),
        P(("grp", "blk"), None, None),
        P(),
    )
    out_specs = (P(("grp", "blk"), None), P(("grp", "blk"), None), P(("blk", "grp"), None))
    return jax.shard_map(
        on_device, mesh=mesh, in_specs=in_specs, out_specs=out_specs, check_vma=False
    )
```

```python
import functools

import jax
import jax.numpy as jnp
from jax import lax
from jax.experimental import pallas as pl
from jax.experimental.pallas import tpu as pltpu
from jax.sharding import PartitionSpec as P

TILE = 128
STEPS = 6
PASSES = 2
GEOM = (4, 4, 8)
YC_OPEN = 4
YC_CLOSE = 2
LANES = 128

momentum_decay = 0.9
shrinkage = 0.05
rate_scale = 0.8

MESH = pl.DeviceIdType.MESH
f32 = jnp.float32
bf16 = jnp.bfloat16


def split2(a):
    hi = a.astype(bf16)
    return hi, (a - hi.astype(f32)).astype(bf16)


def dot3(a, b, dims):
    def one(p, q):
        return lax.dot_general(p, q, (dims, ((), ())), preferred_element_type=f32)

    return one(a[0], b[0]) + (one(a[0], b[1]) + one(a[1], b[0]))


def kernel(
    stag, tiles, users, umom, items, imom, ratings, mask,
    out_u, out_p, out_i,
    own, got, outbox, hold, raw_m, rat, wgt,
    c1_in, c2_out, c2_in, tally,
    load_sem, s1, r1, s2, r2, ring_s, ring_r, sc, rc,
):
    nx, nl, ny = GEOM
    nz = 2 * nl
    ng, nb = nx * nl, ny * 4
    rank = out_u.shape[1]
    halves = rank // LANES
    n_items = own.shape[1]
    n_users = out_u.shape[0]
    planes, prow = got.shape[1], got.shape[2]
    g = lax.axis_index("grp")
    b = lax.axis_index("blk")
    x, y, z, c = g // nl, b // 4, (b // 2) % 2 * nl + g % nl, b % 2

    def dev(xx, yy, zz, cc):
        return (xx * nl + zz % nl, (yy * 2 + zz // nl) * 2 + cc)

    def rows_cols(xx, yy, zz, cc):
        row = ((xx * nl + zz % nl) * 2 + cc) * prow
        col = yy % halves * LANES
        return pl.ds(pl.multiple_of(row, prow), prow), pl.ds(pl.multiple_of(col, LANES), LANES)

    def part(ref, at):
        plane = at[1] % YC_OPEN // halves * planes
        return ref.at[(pl.ds(plane, planes), *rows_cols(*at))]

    loads = []
    for i, (src, dst) in enumerate(
        (
            (items, own.at[0]),
            (imom, own.at[1]),
            (ratings, rat),
            (mask, raw_m),
            (users, out_u),
            (umom, out_p),
        )
    ):
        copy = pltpu.make_async_copy(src, dst, load_sem.at[i])
        copy.start()
        loads.append(copy)

    def pairs(classes, sign):
        found = [((x, y, z, 1 - c), True)]
        for cc in (1, 0):
            for dx in range(nx):
                xx = (x + dx) % nx
                hx, hc = (xx, cc) if sign > 0 else (x, c)
                for dz in range(nl):
                    zoff = dz if 2 * dz < nl else dz - nl
                    if 2 * dz == nl:
                        zoff = dz * (1 - 2 * hc)
                    for dy in range(classes):
                        yoff = dy if 2 * dy < classes else dy - classes
                        if 2 * dy == classes:
                            yoff = dy * (1 - 2 * ((hx + hc) % 2))
                        if dx + dz + dy:
                            yy = (y + sign * yoff + ny) % ny
                            zz = (z + sign * zoff + nz) % nz
                            found.append(((xx, yy, zz, cc), dx + dz == 0))
        return found

    for gg in range(ng):
        c1_in[gg] = jnp.zeros(c1_in.shape[1:], f32)

    barrier = pltpu.get_barrier_semaphore()
    greet = [(g, (b + d) % nb) for d in range(1, nb)]
    greet += [dev(x, yy, nz - 1 - z, cc) for yy in range(ny) for cc in range(2)]
    greet += [dev(*at) for at, near in pairs(YC_OPEN, 1) if not near]
    greet += [dev(*at) for at, near in pairs(YC_CLOSE, -1) if not near]
    for who in greet:
        pl.semaphore_signal(barrier, inc=1, device_id=who, device_id_type=MESH)
    loads[0].wait()
    loads[1].wait()
    pl.semaphore_wait(barrier, len(greet))

    me = (x, y, z, c)
    for dy in sorted(range(ny), key=lambda d: -min(d, ny - d)):
        for flip in range(2):
            for dc in range(2):
                if dy + flip + dc == 0:
                    continue
                at = (x, (y + dy) % ny, (nz - 1 - z if flip else z), (c + dc) % 2)
                pltpu.make_async_remote_copy(
                    src_ref=part(own, at),
                    dst_ref=got.at[b],
                    send_sem=s1,
                    recv_sem=r1,
                    device_id=dev(*at),
                    device_id_type=MESH,
                ).start()
    got[b] = part(own, me)[...]

    for copy in loads[2:]:
        copy.wait()
    for s in range(STEPS):
        for ut in range(n_users // TILE):
            for it in range(n_items // TILE):
                ur, ir = pl.ds(ut * TILE, TILE), pl.ds(it * TILE, TILE)
                wgt[s, ur, ir] = (raw_m[s, ur, ir] * tiles[ut, it, s]).astype(f32)

    several = got.at[pl.ds(0, nb - 1)]
    pltpu.make_async_copy(several, several, r1).wait()

    part(hold.at[0], me)[...] = got[(b + stag[g]) % nb]
    outs = [dev(*at) for at, _ in pairs(YC_OPEN, -1)]
    for k, (gd, bd) in enumerate(outs):
        outbox[k] = got[(bd + stag[gd]) % nb]
    for k, who in enumerate(outs):
        pltpu.make_async_remote_copy(
            src_ref=outbox.at[k],
            dst_ref=part(hold.at[0], me),
            send_sem=s2,
            recv_sem=r2,
            device_id=who,
            device_id_type=MESH,
        ).start()
    sent = outbox.at[pl.ds(0, len(outs))]
    pltpu.make_async_copy(sent, sent, r2).wait()

    def onward(s):
        return pltpu.make_async_remote_copy(
            src_ref=hold.at[s],
            dst_ref=hold.at[s + 1],
            send_sem=ring_s.at[s],
            recv_sem=ring_r.at[s],
            device_id=(g, (b + 1) % nb),
            device_id_type=MESH,
        )

    user_rate = rate_scale / n_items
    item_rate = rate_scale / n_users

    def step(s, carry):
        @pl.when(s > 0)
        def _():
            onward(s - 1).wait_recv()

        for _ in range(PASSES):
            u, v = out_u[...], hold[s, 0]
            us, vs = split2(u), split2(v)
            pred = dot3(us, vs, ((1,), (1,)))
            res = split2(wgt[s] * (pred - rat[s]))
            ugrad = dot3(res, vs, ((1,), (0,))) + shrinkage * u
            igrad = dot3(res, us, ((0,), (0,))) + shrinkage * v
            p = momentum_decay * out_p[...] + ugrad
            m = momentum_decay * hold[s, 1] + igrad
            out_p[...] = p
            out_u[...] = u - user_rate * p
            hold[s, 1] = m
            hold[s, 0] = v - item_rate * m

        @pl.when(s < STEPS - 1)
        def _():
            onward(s).start()

        return carry

    lax.fori_loop(0, STEPS, step, 0)

    last = hold.at[STEPS - 1, 0]
    for at, _ in pairs(YC_CLOSE, 1):
        pltpu.make_async_remote_copy(
            src_ref=last.at[rows_cols(*at)],
            dst_ref=c1_in.at[g, b],
            send_sem=sc.at[0],
            recv_sem=rc.at[0],
            device_id=dev(*at),
            device_id_type=MESH,
        ).start()
    c1_in[g, b] = last[rows_cols(*me)]
    some = tally.at[pl.ds(0, ng * 2 * YC_CLOSE - 1)]
    pltpu.make_async_copy(some, some, rc.at[0]).wait()
    shifts = [nb - stag[gg] + STEPS - 1 for gg in range(ng)]
    for j in range(nb):
        total = c1_in[0, (j + shifts[0]) % nb]
        for gg in range(1, ng):
            total = total + c1_in[gg, (j + shifts[gg]) % nb]
        c2_out[j] = total * (1 / ng)
    for d in sorted(range(1, nb), key=lambda d: -min(d, nb - d)):
        t = (b + d) % nb
        pltpu.make_async_remote_copy(
            src_ref=c2_out.at[t],
            dst_ref=c2_in.at[b],
            send_sem=sc.at[1],
            recv_sem=rc.at[1],
            device_id=(g, t),
            device_id_type=MESH,
        ).start()
    c2_in[b] = c2_out[b]

    pltpu.make_async_copy(several, several, s1).wait()
    pltpu.make_async_copy(sent, sent, s2).wait()
    for s in range(STEPS - 1):
        onward(s).wait_send()
    pltpu.make_async_copy(some, some, sc.at[0]).wait()
    some2 = c2_in.at[pl.ds(0, nb - 1)]
    pltpu.make_async_copy(some2, some2, sc.at[1]).wait()
    pltpu.make_async_copy(some2, some2, rc.at[1]).wait()
    for cc in range(2):
        for h in range(halves):
            held = [c2_in[(yy * 2 + zh) * 2 + cc] for yy in range(h, ny, halves) for zh in range(2)]
            out_i[pl.ds(cc * prow, prow), pl.ds(h * LANES, LANES)] = sum(held[1:], held[0])


def copy_out(*refs):
    n = len(refs) // 2
    for src, dst in zip(refs[:n], refs[n:]):
        dst[...] = src[...]


def on_device(
    users, user_momentum, items, item_momentum, ratings, rating_mask, tile_occupied, stagger
):
    nx, nl, ny = GEOM
    ng, nb = nx * nl, ny * 4
    n_users, rank = users.shape
    n_items = items.shape[0]
    pieces = ng * 2 * YC_OPEN
    planes = 4 // YC_OPEN
    prow = n_items // (ng * 2)
    vm = pl.BlockSpec(memory_space=pltpu.VMEM)
    sm = pl.BlockSpec(memory_space=pltpu.SMEM)
    hbm = pl.BlockSpec(memory_space=pl.ANY)
    dma = pltpu.SemaphoreType.DMA
    results = pl.pallas_call(
        kernel,
        out_shape=(
            jax.ShapeDtypeStruct(users.shape, f32),
            jax.ShapeDtypeStruct(users.shape, f32),
            jax.ShapeDtypeStruct((n_items // ng, rank), f32),
        ),
        in_specs=[sm, sm] + [hbm] * 6,
        out_specs=(vm, vm, vm),
        scratch_shapes=[
            pltpu.VMEM((2, n_items, rank), f32),
            pltpu.VMEM((nb, planes, prow, LANES), f32),
            pltpu.VMEM((pieces, planes, prow, LANES), f32),
            pltpu.VMEM((STEPS, 2, n_items, rank), f32),
            pltpu.VMEM((STEPS, n_users, n_items), jnp.int32),
            pltpu.VMEM((STEPS, n_users, n_items), f32),
            pltpu.VMEM((STEPS, n_users, n_items), f32),
            pltpu.VMEM((ng, nb, prow, LANES), f32),
            pltpu.VMEM((nb, prow, LANES), f32),
            pltpu.VMEM((nb, prow, LANES), f32),
            pltpu.VMEM((ng * 2 * YC_CLOSE, prow, LANES), f32),
            dma((6,)),
            dma,
            dma,
            dma,
            dma,
            dma((STEPS - 1,)),
            dma((STEPS - 1,)),
            dma((2,)),
            dma((2,)),
        ],
        compiler_params=pltpu.CompilerParams(
            collective_id=0, has_side_effects=True, vmem_limit_bytes=60 * 2**20
        ),
        name="window",
    )(
        stagger,
        jnp.transpose(tile_occupied, (0, 2, 1)),
        users,
        user_momentum,
        items,
        item_momentum,
        jnp.transpose(ratings, (1, 0, 2)),
        jnp.transpose(rating_mask, (1, 0, 2)),
    )
    return pl.pallas_call(
        copy_out,
        out_shape=tuple(jax.ShapeDtypeStruct(r.shape, r.dtype) for r in results),
        in_specs=[vm] * 3,
        out_specs=(vm,) * 3,
        name="results",
    )(*results)


def solution(mesh):
    in_specs = (
        P(("grp", "blk"), None),
        P(("grp", "blk"), None),
        P("blk", None),
        P("blk", None),
        P(("grp", "blk"), None, None),
        P(("grp", "blk"), None, None),
        P(("grp", "blk"), None, None),
        P(),
    )
    out_specs = (P(("grp", "blk"), None), P(("grp", "blk"), None), P(("blk", "grp"), None))
    return jax.shard_map(
        on_device, mesh=mesh, in_specs=in_specs, out_specs=out_specs, check_vma=False
    )
```

```python
import functools

import jax
import jax.numpy as jnp
from jax import lax
from jax.experimental import pallas as pl
from jax.experimental.pallas import tpu as pltpu
from jax.sharding import PartitionSpec as P

TILE = 128
STEPS = 6
PASSES = 2
GEOM = (4, 4, 8)
YC_OPEN = 4
YC_CLOSE = 2
LANES = 128

momentum_decay = 0.9
shrinkage = 0.05
rate_scale = 0.8

MESH = pl.DeviceIdType.MESH
f32 = jnp.float32
bf16 = jnp.bfloat16


def split2(a):
    hi = a.astype(bf16)
    return hi, (a - hi.astype(f32)).astype(bf16)


def dot3(a, b, dims):
    def one(p, q):
        return lax.dot_general(p, q, (dims, ((), ())), preferred_element_type=f32)

    return one(a[0], b[0]) + (one(a[0], b[1]) + one(a[1], b[0]))


def kernel(
    stag, tiles, users, umom, items, imom, ratings, mask,
    out_u, out_p, out_i,
    own, got, outbox, hold, raw_m, rat, wgt,
    user, c1_in, c2_out, c2_in, tally,
    load_sem, s1, r1, s2, r2, ring_s, ring_r, sc, rc,
):
    nx, nl, ny = GEOM
    nz = 2 * nl
    ng, nb = nx * nl, ny * 4
    n_users, rank = user.shape[1:]
    halves = rank // LANES
    n_items = own.shape[1]
    planes, prow = got.shape[1], got.shape[2]
    g = lax.axis_index("grp")
    b = lax.axis_index("blk")
    x, y, z, c = g // nl, b // 4, (b // 2) % 2 * nl + g % nl, b % 2

    def dev(xx, yy, zz, cc):
        return (xx * nl + zz % nl, (yy * 2 + zz // nl) * 2 + cc)

    def rows_cols(xx, yy, zz, cc):
        row = ((xx * nl + zz % nl) * 2 + cc) * prow
        col = yy % halves * LANES
        return pl.ds(pl.multiple_of(row, prow), prow), pl.ds(pl.multiple_of(col, LANES), LANES)

    def part(ref, at):
        plane = at[1] % YC_OPEN // halves * planes
        return ref.at[(pl.ds(plane, planes), *rows_cols(*at))]

    loads = []
    for i, (src, dst) in enumerate(
        (
            (items, own.at[0]),
            (imom, own.at[1]),
            (ratings, rat),
            (mask, raw_m),
            (users, user.at[0]),
            (umom, user.at[1]),
        )
    ):
        copy = pltpu.make_async_copy(src, dst, load_sem.at[i])
        copy.start()
        loads.append(copy)

    def pairs(classes, sign):
        found = [((x, y, z, 1 - c), True)]
        for cc in (1, 0):
            for dx in range(nx):
                xx = (x + dx) % nx
                hx, hc = (xx, cc) if sign > 0 else (x, c)
                for dz in range(nl):
                    zoff = dz if 2 * dz < nl else dz - nl
                    if 2 * dz == nl:
                        zoff = dz * (1 - 2 * hc)
                    for dy in range(classes):
                        yoff = dy if 2 * dy < classes else dy - classes
                        if 2 * dy == classes:
                            yoff = dy * (1 - 2 * ((hx + hc) % 2))
                        if dx + dz + dy:
                            yy = (y + sign * yoff + ny) % ny
                            zz = (z + sign * zoff + nz) % nz
                            found.append(((xx, yy, zz, cc), dx + dz == 0))
        return found

    for gg in range(ng):
        c1_in[gg] = jnp.zeros(c1_in.shape[1:], f32)

    barrier = pltpu.get_barrier_semaphore()
    greet = [(g, (b + d) % nb) for d in range(1, nb)]
    greet += [dev(x, yy, nz - 1 - z, cc) for yy in range(ny) for cc in range(2)]
    greet += [dev(*at) for at, near in pairs(YC_OPEN, 1) if not near]
    for who in greet:
        pl.semaphore_signal(barrier, inc=1, device_id=who, device_id_type=MESH)
    loads[0].wait()
    loads[1].wait()
    pl.semaphore_wait(barrier, len(greet))

    me = (x, y, z, c)
    for dy in sorted(range(ny), key=lambda d: -min(d, ny - d)):
        for flip in range(2):
            for dc in range(2):
                if dy + flip + dc == 0:
                    continue
                at = (x, (y + dy) % ny, (nz - 1 - z if flip else z), (c + dc) % 2)
                pltpu.make_async_remote_copy(
                    src_ref=part(own, at),
                    dst_ref=got.at[b],
                    send_sem=s1,
                    recv_sem=r1,
                    device_id=dev(*at),
                    device_id_type=MESH,
                ).start()
    got[b] = part(own, me)[...]

    for copy in loads[2:]:
        copy.wait()
    for s in range(STEPS):
        for ut in range(n_users // TILE):
            for it in range(n_items // TILE):
                ur, ir = pl.ds(ut * TILE, TILE), pl.ds(it * TILE, TILE)
                wgt[s, ur, ir] = (raw_m[s, ur, ir] * tiles[ut, it, s]).astype(f32)

    several = got.at[pl.ds(0, nb - 1)]
    pltpu.make_async_copy(several, several, r1).wait()

    part(hold.at[0], me)[...] = got[(b + stag[g]) % nb]
    outs = [dev(*at) for at, _ in pairs(YC_OPEN, -1)]
    for k, (gd, bd) in enumerate(outs):
        outbox[k] = got[(bd + stag[gd]) % nb]
    for k, who in enumerate(outs):
        pltpu.make_async_remote_copy(
            src_ref=outbox.at[k],
            dst_ref=part(hold.at[0], me),
            send_sem=s2,
            recv_sem=r2,
            device_id=who,
            device_id_type=MESH,
        ).start()
    sent = outbox.at[pl.ds(0, len(outs))]
    pltpu.make_async_copy(sent, sent, r2).wait()

    def onward(s):
        return pltpu.make_async_remote_copy(
            src_ref=hold.at[s],
            dst_ref=hold.at[s + 1],
            send_sem=ring_s.at[s],
            recv_sem=ring_r.at[s],
            device_id=(g, (b + 1) % nb),
            device_id_type=MESH,
        )

    user_rate = rate_scale / n_items
    item_rate = rate_scale / n_users

    last = hold.at[STEPS - 1, 0]

    def give():
        for at, _ in pairs(YC_CLOSE, 1):
            pltpu.make_async_remote_copy(
                src_ref=last.at[rows_cols(*at)],
                dst_ref=c1_in.at[g, b],
                send_sem=sc.at[0],
                recv_sem=rc.at[0],
                device_id=dev(*at),
                device_id_type=MESH,
            ).start()

    def step(s, carry):
        @pl.when(s > 0)
        def _():
            onward(s - 1).wait_recv()

        for again in range(PASSES):
            u, v = user[0], hold[s, 0]
            us, vs = split2(u), split2(v)
            pred = dot3(us, vs, ((1,), (1,)))
            res = split2(wgt[s] * (pred - rat[s]))
            igrad = dot3(res, us, ((0,), (0,))) + shrinkage * v
            m = momentum_decay * hold[s, 1] + igrad
            hold[s, 1] = m
            hold[s, 0] = v - item_rate * m
            if again == PASSES - 1:

                @pl.when(s < STEPS - 1)
                def _():
                    onward(s).start()

                @pl.when(s == STEPS - 1)
                def _():
                    give()

            ugrad = dot3(res, vs, ((1,), (0,))) + shrinkage * u
            p = momentum_decay * user[1] + ugrad
            user[1] = p
            user[0] = u - user_rate * p

        return carry

    lax.fori_loop(0, STEPS, step, 0)
    stores = []
    for i, dst in enumerate((out_u, out_p)):
        copy = pltpu.make_async_copy(user.at[i], dst, load_sem.at[i])
        copy.start()
        stores.append(copy)
    c1_in[g, b] = last[rows_cols(*me)]
    some = tally.at[pl.ds(0, ng * 2 * YC_CLOSE - 1)]
    pltpu.make_async_copy(some, some, rc.at[0]).wait()
    shifts = [nb - stag[gg] + STEPS - 1 for gg in range(ng)]

    def block_sum(j):
        total = c1_in[0, (j + shifts[0]) % nb]
        for gg in range(1, ng):
            total = total + c1_in[gg, (j + shifts[gg]) % nb]
        return total * (1 / ng)

    waiting = []
    for d in [*sorted(range(1, nb), key=lambda d: -min(d, nb - d)), 0, 0, 0]:
        if len(waiting) == 3 or d == 0:
            t = waiting.pop(0)
            pltpu.make_async_remote_copy(
                src_ref=c2_out.at[t],
                dst_ref=c2_in.at[b],
                send_sem=sc.at[1],
                recv_sem=rc.at[1],
                device_id=(g, t),
                device_id_type=MESH,
            ).start()
        if d:
            j = (b + d) % nb
            waiting.append(j)
            c2_out[j] = block_sum(j)
    c2_in[b] = block_sum(b)

    for copy in stores:
        copy.wait()
    pltpu.make_async_copy(several, several, s1).wait()
    pltpu.make_async_copy(sent, sent, s2).wait()
    for s in range(STEPS - 1):
        onward(s).wait_send()
    pltpu.make_async_copy(some, some, sc.at[0]).wait()
    some2 = c2_in.at[pl.ds(0, nb - 1)]
    pltpu.make_async_copy(some2, some2, sc.at[1]).wait()
    pltpu.make_async_copy(some2, some2, rc.at[1]).wait()
    for cc in range(2):
        for h in range(halves):
            held = [c2_in[(yy * 2 + zh) * 2 + cc] for yy in range(h, ny, halves) for zh in range(2)]
            out_i[pl.ds(cc * prow, prow), pl.ds(h * LANES, LANES)] = sum(held[1:], held[0])


def copy_out(*refs):
    n = len(refs) // 3
    sources, results, held, sem = refs[:n], refs[n : 2 * n], refs[2 * n : 3 * n], refs[-1]
    ins = [pltpu.make_async_copy(r, h, sem.at[i]) for i, (r, h) in enumerate(zip(sources, held))]
    outs = [pltpu.make_async_copy(h, r, sem.at[n + i]) for i, (h, r) in enumerate(zip(held, results))]
    for copy in ins:
        copy.start()
    for come, go in zip(ins, outs):
        come.wait()
        go.start()
    for copy in outs:
        copy.wait()


def on_device(
    users, user_momentum, items, item_momentum, ratings, rating_mask, tile_occupied, stagger
):
    nx, nl, ny = GEOM
    ng, nb = nx * nl, ny * 4
    n_users, rank = users.shape
    n_items = items.shape[0]
    pieces = ng * 2 * YC_OPEN
    planes = 4 // YC_OPEN
    prow = n_items // (ng * 2)
    vm = pl.BlockSpec(memory_space=pltpu.VMEM)
    sm = pl.BlockSpec(memory_space=pltpu.SMEM)
    hbm = pl.BlockSpec(memory_space=pl.ANY)
    dma = pltpu.SemaphoreType.DMA
    results = pl.pallas_call(
        kernel,
        out_shape=(
            jax.ShapeDtypeStruct(users.shape, f32),
            jax.ShapeDtypeStruct(users.shape, f32),
            jax.ShapeDtypeStruct((n_items // ng, rank), f32),
        ),
        in_specs=[sm, sm] + [hbm] * 6,
        out_specs=(hbm, hbm, vm),
        scratch_shapes=[
            pltpu.VMEM((2, n_items, rank), f32),
            pltpu.VMEM((nb, planes, prow, LANES), f32),
            pltpu.VMEM((pieces, planes, prow, LANES), f32),
            pltpu.VMEM((STEPS, 2, n_items, rank), f32),
            pltpu.VMEM((STEPS, n_users, n_items), jnp.int32),
            pltpu.VMEM((STEPS, n_users, n_items), f32),
            pltpu.VMEM((STEPS, n_users, n_items), f32),
            pltpu.VMEM((2, n_users, rank), f32),
            pltpu.VMEM((ng, nb, prow, LANES), f32),
            pltpu.VMEM((nb, prow, LANES), f32),
            pltpu.VMEM((nb, prow, LANES), f32),
            pltpu.VMEM((ng * 2 * YC_CLOSE, prow, LANES), f32),
            dma((6,)),
            dma,
            dma,
            dma,
            dma,
            dma((STEPS - 1,)),
            dma((STEPS - 1,)),
            dma((2,)),
            dma((2,)),
        ],
        compiler_params=pltpu.CompilerParams(
            collective_id=0, has_side_effects=True, vmem_limit_bytes=60 * 2**20
        ),
        name="window",
    )(
        stagger,
        jnp.transpose(tile_occupied, (0, 2, 1)),
        users,
        user_momentum,
        items,
        item_momentum,
        jnp.transpose(ratings, (1, 0, 2)),
        jnp.transpose(rating_mask, (1, 0, 2)),
    )
    return pl.pallas_call(
        copy_out,
        out_shape=tuple(jax.ShapeDtypeStruct(r.shape, r.dtype) for r in results),
        in_specs=[hbm] * 3,
        out_specs=(hbm,) * 3,
        scratch_shapes=[*(pltpu.VMEM(r.shape, r.dtype) for r in results), dma((6,))],
        compiler_params=pltpu.CompilerParams(vmem_limit_bytes=60 * 2**20),
        name="results",
    )(*results)


def solution(mesh):
    in_specs = (
        P(("grp", "blk"), None),
        P(("grp", "blk"), None),
        P("blk", None),
        P("blk", None),
        P(("grp", "blk"), None, None),
        P(("grp", "blk"), None, None),
        P(("grp", "blk"), None, None),
        P(),
    )
    out_specs = (P(("grp", "blk"), None), P(("grp", "blk"), None), P(("blk", "grp"), None))
    return jax.shard_map(
        on_device, mesh=mesh, in_specs=in_specs, out_specs=out_specs, check_vma=False
    )
```
